512 devices in a mesh: grp: 2 (over x_hi), dp: 16 (over x_lo, z), mp: 16 (over y, core).
Axes of the slice: x: 4 (x_hi: 2, x_lo: 2; x = x_hi * 2 + x_lo), y: 8, z: 8, core: 2. Of those that a mesh axis runs over, the one named last changes fastest.
Arguments:
- captured: bfloat16 [3, 1024, 8192], P(None, 'mp', ('grp', 'dp')), may hold values from -9 to 9
- unite_weight: bfloat16 [3, 8192, 8192], P(None, ('grp', 'dp'), 'mp'), may hold values from -0.0390625 to 0.0390625
- heads: bfloat16 [2, 16000, 8192], P('grp', 'dp', 'mp'), may hold values from -10 to 10, as said below
- final_hidden: bfloat16 [1024, 8192], P('dp', 'mp'), may hold values from -9 to 9
- target_gain: float32 [8192], P('mp'), may hold values from 0.1 to 1.9
- draft_gain: float32 [8192], P('mp'), may hold values from 0.1 to 1.9
- lengths: int32 [16], replicated, may hold values from 32 to 64
Outputs:
- grad_terms: bfloat16 [2, 16000, 8192], P('grp', 'dp', 'mp')
- token_loss: float32 [1024], P('mp')
The draws below stay inside these ranges and needn't reach their ends.
Inputs may be any that keep to these rules, and one draw needn't show every extreme that they name: `heads`: each row of a head has its own scale.
All inputs are finite; a program needn't handle non-finite values.
Results may differ from the reference program's by a relative error of at most 0.0051.
Values may be sent and summed in bfloat16 or wider, within the bound.
No kernel may reach another device: no remote copies, remote signals or barrier semaphores. Data moves between devices by JAX's collectives and lax.ppermute only.
A program may use at most 64 MiB of HBM per device.

```python
import math
import jax
import jax.numpy as jnp
from jax import lax

D = 8192
DV = 16000
LAYERS = 3
TOK_DEV = 64
SLABS = 16
TOKENS = 1024


def draw_heads(key, part):
    normal_key, scale_key = jax.random.split(jax.random.fold_in(key, 11), 2)
    normal_base = jnp.clip(jax.random.normal(normal_key, (2, DV, D), jnp.float32), -6.0, 6.0) / math.sqrt(D)
    row_scale = jnp.exp(jax.random.uniform(scale_key, (2, DV, 1), jnp.float32, math.log(0.2), math.log(2.5)))
    return jnp.clip(normal_base * row_scale, -10.0, 10.0).astype(jnp.bfloat16)


def common_direction(key, amp_low, amp_high):
    direction_key, amplitude_key = jax.random.split(jax.random.fold_in(key, 29), 2)
    direction = jnp.clip(jax.random.normal(direction_key, (D,), jnp.float32), -3.0, 3.0)
    amplitude = jax.random.uniform(amplitude_key, (TOKENS,), jnp.float32, amp_low, amp_high)
    return (direction, amplitude)


def draw_final_hidden(key, part):
    noise_key = jax.random.fold_in(key, 31)
    direction, amplitude = common_direction(key, 0.4, 1.2)
    noise = jnp.clip(jax.random.normal(noise_key, (TOKENS, D), jnp.float32), -6.0, 6.0)
    values = noise + 0.8 * amplitude[:, None] * direction[None, :]
    return values.astype(jnp.bfloat16)


def draw_captured(key, part):
    noise_key = jax.random.fold_in(key, 37)
    direction, amplitude = common_direction(key, 0.4, 1.2)
    noise = jnp.clip(jax.random.normal(noise_key, (LAYERS, TOKENS, D), jnp.float32), -6.0, 6.0)
    values = noise + 0.8 * amplitude[None, :, None] * direction[None, None, :]
    return values.astype(jnp.bfloat16)


def with_ends(result, rng, smallest, largest):
    place = [jax.random.randint(jax.random.fold_in(rng, axis), (), 0, length) for axis, length in enumerate(result.shape)]
    main_axis = result.shape.index(max(result.shape))
    beside = place[:main_axis] + [(place[main_axis] + 1) % result.shape[main_axis]] + place[main_axis + 1:]
    return result.at[tuple(place)].set(smallest).at[tuple(beside)].set(largest)


def level_of(rng, shape, cuts, low, high):
    def one(axis_at, blocks):
        draws = jax.random.uniform(jax.random.fold_in(jax.random.fold_in(rng, 6), axis_at), (blocks,), jnp.float32, low / len(cuts), high / len(cuts))
        return jnp.repeat(jnp.exp(draws), shape[axis_at] // blocks).reshape((-1,) + (1,) * (len(shape) - axis_at - 1))

    loudness = one(*cuts[0])
    for cut in cuts[1:]:
        loudness = loudness * one(*cut)
    return loudness


def centred(rng, dims, width, reach, cuts=(), held_as=jnp.bfloat16):
    result = width * jax.random.normal(rng, dims, jnp.float32)
    if cuts:
        result = result * level_of(rng, dims, cuts, -0.22, 0.18)
    return jnp.clip(result, -reach, reach).astype(held_as)


def setup_inputs(seed: int = 0) -> dict:
    key_of = jax.random.split(jax.random.key(seed), 8)
    captured = draw_captured(jax.random.fold_in(key_of[7], 71), 0)
    unite_weight = centred(key_of[1], (LAYERS, D, D), (LAYERS * D) ** -0.5, 0.0390625, ((1, 32), (2, 16)))
    heads = draw_heads(jax.random.fold_in(key_of[7], 71), 0)
    final_hidden = draw_final_hidden(jax.random.fold_in(key_of[7], 71), 0)
    target_gain = jnp.clip(1.0 + 0.18 * jax.random.normal(key_of[4], (D,), jnp.float32), 0.1, 1.9)
    draft_gain = jnp.clip(1.0 + 0.18 * jax.random.normal(key_of[5], (D,), jnp.float32), 0.1, 1.9)
    lengths = with_ends(jax.random.randint(key_of[6], (SLABS,), TOK_DEV // 2, TOK_DEV + 1), jax.random.fold_in(key_of[6], 1), TOK_DEV // 2, TOK_DEV).astype(jnp.int32)
    return {"captured": captured, "unite_weight": unite_weight, "heads": heads, "final_hidden": final_hidden, "target_gain": target_gain, "draft_gain": draft_gain, "lengths": lengths}


EPSILON = 1e-05

def normalize(row_values, gain_vector):
    values = row_values.astype(jnp.float32)
    inverse_rms = lax.rsqrt(lax.optimization_barrier(jnp.mean(values * values, axis=1, keepdims=True)) + EPSILON)
    return (values * inverse_rms * gain_vector[None, :]).astype(jnp.bfloat16)

def united_features(captured, unite_weight):
    summed = jnp.dot(captured[0], unite_weight[0], preferred_element_type=jnp.float32)
    for layer_index in range(1, LAYERS):
        summed = summed + jnp.dot(captured[layer_index], unite_weight[layer_index], preferred_element_type=jnp.float32)
    return summed

def vocab_logits(row_values, head_rows):
    return jnp.dot(row_values, head_rows.T, preferred_element_type=jnp.float32)

def softmax_parts(logits):
    row_max = lax.optimization_barrier(jnp.max(logits, axis=1, keepdims=True))
    shifted = logits - row_max
    row_total = lax.optimization_barrier(jnp.sum(jnp.exp(shifted), axis=1, keepdims=True))
    return (jnp.exp(shifted) / row_total, shifted - jnp.log(row_total))

def reference(captured, unite_weight, heads, final_hidden, target_gain, draft_gain, lengths):
    united = united_features(captured, unite_weight)
    draft_rows = normalize(united, draft_gain)
    target_rows = normalize(final_hidden, target_gain)
    target_probs, unused_logs = softmax_parts(vocab_logits(target_rows, heads[0]))
    draft_probs, draft_logs = softmax_parts(vocab_logits(draft_rows, heads[1]))
    token_index = jnp.arange(TOKENS, dtype=jnp.int32)
    slab_index = token_index // TOK_DEV
    position = token_index - slab_index * TOK_DEV
    valid_mask = (position < lengths[slab_index]).astype(jnp.float32)
    valid_total = jnp.sum(lengths).astype(jnp.float32)
    token_loss = -valid_mask * lax.optimization_barrier(jnp.sum(target_probs * draft_logs, axis=1))
    weights = (valid_mask / valid_total)[:, None]
    target_weighted = (target_probs * weights).astype(jnp.bfloat16)
    delta_weighted = ((draft_probs - target_probs) * weights).astype(jnp.bfloat16)
    target_term = jnp.dot(target_weighted.T, draft_rows, preferred_element_type=jnp.float32)
    delta_term = jnp.dot(delta_weighted.T, draft_rows, preferred_element_type=jnp.float32)
    grad_terms = jnp.stack([(-target_term).astype(jnp.bfloat16), delta_term.astype(jnp.bfloat16)])
    return (grad_terms, token_loss)
```

```python
import jax
import jax.numpy as jnp
from jax import lax
from jax.sharding import Mesh, PartitionSpec as P

EPSILON = 1e-05
SLABS = ("xl", "z")
BLOCKS = ("grp", "xl", "z")
COLUMNS = ("y", "core")


def exchanged(tiles, axes):
    return lax.all_to_all(tiles, axes, split_axis=0, concat_axis=0, tiled=True)


def copied(shard, axes):
    return exchanged(jnp.broadcast_to(shard, (lax.axis_size(axes), *shard.shape)), axes)


def from_other_core(shard):
    return lax.ppermute(shard, "core", [(0, 1), (1, 0)])


def from_other_group(shard):
    return lax.ppermute(shard, "grp", [(0, 1), (1, 0)])


def per_device(captured, unite_weight, heads, final_hidden, target_gain, draft_gain, lengths):
    f32, bf16, half = jnp.float32, jnp.bfloat16, jnp.float16
    columns = final_hidden.shape[1]
    model_width = columns * lax.axis_size(COLUMNS)
    layers, slab, features = captured.shape
    n_y = lax.axis_size("y")
    n_slabs = lax.axis_size(SLABS)
    part = slab // 2
    group = lax.axis_index("grp")
    core = lax.axis_index("core")
    is_target = group == 0
    is_first = core == 0
    vocab = heads.shape[1]

    own_heads = heads[0]
    other_heads = from_other_group(own_heads)
    both_heads = jnp.stack(
        [
            jnp.where(is_target, own_heads, other_heads),
            jnp.where(is_target, other_heads, own_heads),
        ]
    )
    core_heads = from_other_core(both_heads)

    hidden_part = jnp.where(is_target, final_hidden[:part], final_hidden[part:])
    hidden_rows = copied(hidden_part, SLABS).astype(f32)

    block = captured.transpose(1, 0, 2).reshape(slab, layers * features)
    mine = copied(block, "y")
    other = from_other_core(mine)
    tokens = jnp.stack(
        [jnp.where(is_first, mine, other), jnp.where(is_first, other, mine)], axis=1
    ).reshape(-1, layers * features)
    partial = jnp.dot(
        tokens, unite_weight.reshape(layers * features, columns), preferred_element_type=f32
    )
    pieces = partial.astype(half).reshape(n_slabs, 2, part, columns).transpose(1, 0, 2, 3)
    received = exchanged(pieces.reshape(-1, part, columns), BLOCKS)
    united = jnp.sum(received.astype(f32), axis=0)

    squares = jnp.concatenate(
        [
            jnp.sum(united * united, axis=1),
            jnp.sum(hidden_rows * hidden_rows, axis=2).reshape(-1),
        ]
    )
    square_sums = jnp.sum(copied(squares, COLUMNS), axis=0)
    scales = lax.rsqrt(square_sums / model_width + EPSILON)
    draft_part = (united * scales[:part, None] * draft_gain[None, :]).astype(bf16)
    draft_rows = copied(draft_part, SLABS)
    hidden_scale = scales[part:].reshape(n_slabs, part, 1)
    target_rows = (hidden_rows * hidden_scale * target_gain[None, None, :]).astype(bf16)

    def logits_of(rows, which):
        by_core = rows.reshape(n_y, 2, part, columns)
        kept = jnp.where(is_first, by_core[:, 0], by_core[:, 1])
        given = jnp.where(is_first, by_core[:, 1], by_core[:, 0])
        taken = from_other_core(given)
        sums = jnp.einsum(
            "ytd,vd->ytv", kept, both_heads[which], preferred_element_type=f32
        ) + jnp.einsum("ytd,vd->ytv", taken, core_heads[which], preferred_element_type=f32)
        return jnp.sum(exchanged(sums.astype(half), "y").astype(f32), axis=0)

    def row_stats(logits):
        top = jnp.max(logits, axis=1)
        return top, jnp.sum(jnp.exp(logits - top[:, None]), axis=1)

    def combined(tops, totals):
        top = jnp.max(tops, axis=0)
        return top, jnp.sum(totals * jnp.exp(tops - top[None]), axis=0)

    target_logits = logits_of(target_rows, 0)
    target_stats = copied(jnp.stack(row_stats(target_logits)), SLABS)
    target_top, target_total = combined(target_stats[:, 0], target_stats[:, 1])
    target_probs = jnp.exp(target_logits - target_top[:, None]) / target_total[:, None]

    draft_logits = logits_of(draft_rows, 1)
    top, total = row_stats(draft_logits)
    crossed = jnp.sum(target_probs * (draft_logits - top[:, None]), axis=1)
    mass = jnp.sum(target_probs, axis=1)
    stats = copied(jnp.stack([top, total, crossed, mass]), SLABS)
    draft_top, draft_total = combined(stats[:, 0], stats[:, 1])
    draft_probs = jnp.exp(draft_logits - draft_top[:, None]) / draft_total[:, None]
    shift = stats[:, 0] - draft_top[None] - jnp.log(draft_total)[None]
    cross_term = jnp.sum(stats[:, 2] + stats[:, 3] * shift, axis=0)

    slab_index = lax.axis_index("y") * 2 + core
    position = group * part + lax.iota(jnp.int32, part)
    valid_len = jnp.sum(
        jnp.where(lax.iota(jnp.int32, lengths.shape[0]) == slab_index, lengths, 0)
    )
    valid_mask = (position < valid_len).astype(f32)
    valid_total = jnp.sum(lengths).astype(f32)
    own_loss = -valid_mask * cross_term
    other_loss = from_other_group(own_loss)
    token_loss = jnp.concatenate(
        [jnp.where(is_target, own_loss, other_loss), jnp.where(is_target, other_loss, own_loss)]
    )

    weights = (valid_mask / valid_total)[:, None]
    weighted = (target_probs * weights).astype(bf16)
    delta = ((draft_probs - target_probs) * weights).astype(bf16)
    outgoing = jnp.concatenate(
        [
            jnp.broadcast_to(weighted, (n_y, part, vocab)),
            jnp.broadcast_to(delta, (n_y, part, vocab)),
        ]
    )
    gathered = exchanged(outgoing, ("grp", "y"))
    core_gathered = from_other_core(gathered)

    other_rows = from_other_group(draft_rows)
    all_rows = jnp.stack(
        [
            jnp.where(is_target, draft_rows, other_rows),
            jnp.where(is_target, other_rows, draft_rows),
        ]
    ).reshape(2, n_y, 2, part, columns)
    own_side = jnp.where(is_first, all_rows[:, :, 0], all_rows[:, :, 1])
    core_side = jnp.where(is_first, all_rows[:, :, 1], all_rows[:, :, 0])

    def gradient(weights_by_token, rows_by_token):
        return jnp.einsum(
            "tv,td->vd",
            weights_by_token.reshape(-1, vocab),
            rows_by_token.reshape(-1, columns),
            preferred_element_type=f32,
        )

    summed = gradient(gathered, own_side) + gradient(core_gathered, core_side)
    sign_factor = jnp.where(is_target, -1.0, 1.0).astype(f32)
    grad_terms = (sign_factor * summed).astype(bf16)[None]
    return (grad_terms, token_loss)


def solution(mesh):
    sizes = mesh.shape
    grid = mesh.devices.reshape(sizes["grp"], 2, sizes["dp"] // 2, sizes["mp"] // 2, 2)
    fine = Mesh(grid, ("grp", "xl", "z", "y", "core"))
    in_specs = (
        P(None, COLUMNS, BLOCKS),
        P(None, BLOCKS, COLUMNS),
        P("grp", SLABS, COLUMNS),
        P(SLABS, COLUMNS),
        P(COLUMNS),
        P(COLUMNS),
        P(),
    )
    out_specs = (P("grp", SLABS, COLUMNS), P(COLUMNS))
    return jax.shard_map(
        per_device, mesh=fine, in_specs=in_specs, out_specs=out_specs, check_vma=False
    )
```

```python
import jax
import jax.numpy as jnp
from jax import lax
from jax.sharding import Mesh, PartitionSpec as P

EPSILON = 1e-05
SLABS = ("xl", "z")
BLOCKS = ("grp", "xl", "z")
COLUMNS = ("y", "core")


def exchanged(tiles, axes):
    return lax.all_to_all(tiles, axes, split_axis=0, concat_axis=0, tiled=True)


def copied(shard, axes):
    return exchanged(jnp.broadcast_to(shard, (lax.axis_size(axes), *shard.shape)), axes)


def from_other_core(shard):
    return lax.ppermute(shard, "core", [(0, 1), (1, 0)])


def from_other_group(shard):
    return lax.ppermute(shard, "grp", [(0, 1), (1, 0)])


def per_device(captured, unite_weight, heads, final_hidden, target_gain, draft_gain, lengths):
    f32, bf16, half = jnp.float32, jnp.bfloat16, jnp.float16
    columns = final_hidden.shape[1]
    model_width = columns * lax.axis_size(COLUMNS)
    layers, slab, features = captured.shape
    n_y = lax.axis_size("y")
    n_slabs = lax.axis_size(SLABS)
    part = slab // 2
    group = lax.axis_index("grp")
    core = lax.axis_index("core")
    is_target = group == 0
    is_first = core == 0
    vocab = heads.shape[1]

    own_heads = heads[0]
    other_heads = from_other_group(own_heads)
    both_heads = jnp.stack(
        [
            jnp.where(is_target, own_heads, other_heads),
            jnp.where(is_target, other_heads, own_heads),
        ]
    )
    core_heads = from_other_core(both_heads)

    hidden_part = jnp.where(is_target, final_hidden[:part], final_hidden[part:]).astype(f32)

    block = captured.transpose(1, 0, 2).reshape(slab, layers * features)
    mine = copied(block, "y")
    other = from_other_core(mine)
    tokens = jnp.stack(
        [jnp.where(is_first, mine, other), jnp.where(is_first, other, mine)], axis=1
    ).reshape(-1, layers * features)
    partial = jnp.dot(
        tokens, unite_weight.reshape(layers * features, columns), preferred_element_type=f32
    )
    pieces = partial.astype(half).reshape(n_slabs, 2, part, columns).transpose(1, 0, 2, 3)
    received = exchanged(pieces.reshape(-1, part, columns), BLOCKS)
    united = jnp.sum(received.astype(f32), axis=0)

    squares = jnp.stack(
        [jnp.sum(hidden_part * hidden_part, axis=1), jnp.sum(united * united, axis=1)]
    )
    square_sums = jnp.sum(copied(squares, COLUMNS), axis=0)
    scales = lax.rsqrt(square_sums / model_width + EPSILON)
    target_part = (hidden_part * scales[0][:, None] * target_gain[None, :]).astype(bf16)
    draft_part = (united * scales[1][:, None] * draft_gain[None, :]).astype(bf16)
    both_rows = copied(jnp.stack([target_part, draft_part]), SLABS)
    draft_rows = both_rows[:, 1]
    other_rows = from_other_group(draft_rows)

    by_core = both_rows.reshape(n_y, 2, 2, part, columns)
    kept = jnp.where(is_first, by_core[:, 0], by_core[:, 1])
    given = jnp.where(is_first, by_core[:, 1], by_core[:, 0])
    taken = from_other_core(given)

    def partial_logits(which):
        return (
            jnp.einsum(
                "ytd,vd->ytv", kept[:, which], both_heads[which], preferred_element_type=f32
            )
            + jnp.einsum(
                "ytd,vd->ytv", taken[:, which], core_heads[which], preferred_element_type=f32
            )
        ).astype(half)

    partials = jnp.stack([partial_logits(0), partial_logits(1)], axis=1)
    partials = exchanged(partials, "y")
    logits = jnp.sum(partials.astype(f32), axis=0)

    local_top = jnp.max(logits, axis=2)
    shifted = logits - local_top[:, :, None]
    raised = jnp.exp(shifted)
    local_total = jnp.sum(raised, axis=2)
    crossed = jnp.sum(raised[0] * shifted[1], axis=1)
    stats = copied(jnp.concatenate([local_top, local_total, crossed[None]]), BLOCKS)
    stats = stats.reshape(2, n_slabs, 5, part)
    tops, totals, crosses = stats[:, :, 0:2], stats[:, :, 2:4], stats[:, :, 4]
    top = jnp.max(tops, axis=1)
    total = jnp.sum(totals * jnp.exp(tops - top[:, None]), axis=1)
    block_factor = jnp.exp(tops[:, :, 0] - top[:, None, 0]) / total[:, None, 0]
    draft_shift = tops[:, :, 1] - top[:, None, 1] - jnp.log(total)[:, None, 1]
    cross_term = jnp.sum(
        block_factor * (crosses + totals[:, :, 0] * draft_shift), axis=1
    ).reshape(-1)
    own_top = jnp.where(is_target, top[0], top[1])
    own_total = jnp.where(is_target, total[0], total[1])
    probs = jnp.exp(logits - own_top[:, :, None]) / own_total[:, :, None]

    slab_index = lax.axis_index("y") * 2 + core
    valid_len = jnp.sum(
        jnp.where(lax.iota(jnp.int32, lengths.shape[0]) == slab_index, lengths, 0)
    )
    valid_mask = (lax.iota(jnp.int32, slab) < valid_len).astype(f32)
    valid_total = jnp.sum(lengths).astype(f32)
    token_loss = -valid_mask * cross_term

    weights = jnp.where(is_target, valid_mask[:part], valid_mask[part:]) / valid_total
    weighted = (probs[0] * weights[:, None]).astype(bf16)
    delta = ((probs[1] - probs[0]) * weights[:, None]).astype(bf16)
    outgoing = jnp.concatenate(
        [
            jnp.broadcast_to(weighted, (n_y, part, vocab)),
            jnp.broadcast_to(delta, (n_y, part, vocab)),
        ]
    )
    gathered = exchanged(outgoing, ("grp", "y"))
    core_gathered = from_other_core(gathered)

    all_rows = jnp.stack(
        [
            jnp.where(is_target, draft_rows, other_rows),
            jnp.where(is_target, other_rows, draft_rows),
        ]
    ).reshape(2, n_y, 2, part, columns)
    own_side = jnp.where(is_first, all_rows[:, :, 0], all_rows[:, :, 1])
    core_side = jnp.where(is_first, all_rows[:, :, 1], all_rows[:, :, 0])

    def gradient(weights_by_token, rows_by_token):
        return jnp.einsum(
            "tv,td->vd",
            weights_by_token.reshape(-1, vocab),
            rows_by_token.reshape(-1, columns),
            preferred_element_type=f32,
        )

    summed = gradient(gathered, own_side) + gradient(core_gathered, core_side)
    sign_factor = jnp.where(is_target, -1.0, 1.0).astype(f32)
    grad_terms = (sign_factor * summed).astype(bf16)[None]
    return (grad_terms, token_loss)


def solution(mesh):
    sizes = mesh.shape
    grid = mesh.devices.reshape(sizes["grp"], 2, sizes["dp"] // 2, sizes["mp"] // 2, 2)
    fine = Mesh(grid, ("grp", "xl", "z", "y", "core"))
    in_specs = (
        P(None, COLUMNS, BLOCKS),
        P(None, BLOCKS, COLUMNS),
        P("grp", SLABS, COLUMNS),
        P(SLABS, COLUMNS),
        P(COLUMNS),
        P(COLUMNS),
        P(),
    )
    out_specs = (P("grp", SLABS, COLUMNS), P(COLUMNS))
    return jax.shard_map(
        per_device, mesh=fine, in_specs=in_specs, out_specs=out_specs, check_vma=False
    )
```

```python
import jax
import jax.numpy as jnp
from jax import lax
from jax.sharding import Mesh, PartitionSpec as P

EPSILON = 1e-05
SLABS = ("xl", "z")
BLOCKS = ("grp", "xl", "z")
COLUMNS = ("y", "core")


def exchanged(tiles, axes):
    return lax.all_to_all(tiles, axes, split_axis=0, concat_axis=0, tiled=True)


def copied(shard, axes):
    return exchanged(jnp.broadcast_to(shard, (lax.axis_size(axes), *shard.shape)), axes)


def from_other_core(shard):
    return lax.ppermute(shard, "core", [(0, 1), (1, 0)])


def from_other_group(shard):
    return lax.ppermute(shard, "grp", [(0, 1), (1, 0)])


def along_x(shard, step):
    n = lax.axis_size(("grp", "xl"))
    return lax.ppermute(shard, ("grp", "xl"), [(i, (i + step) % n) for i in range(n)])


def per_device(captured, unite_weight, heads, final_hidden, target_gain, draft_gain, lengths):
    f32, bf16, half = jnp.float32, jnp.bfloat16, jnp.float16
    columns = final_hidden.shape[1]
    model_width = columns * lax.axis_size(COLUMNS)
    layers, slab, features = captured.shape
    n_y = lax.axis_size("y")
    n_slabs = lax.axis_size(SLABS)
    part = slab // 2
    group = lax.axis_index("grp")
    core = lax.axis_index("core")
    is_target = group == 0
    is_first = core == 0
    vocab = heads.shape[1]

    own_heads = heads[0]
    first_half, second_half = own_heads[: vocab // 2], own_heads[vocab // 2 :]
    first_half = along_x(first_half, 1)
    second_half = along_x(second_half, -1)
    first_half = along_x(first_half, 1)
    second_half = along_x(second_half, -1)
    other_heads = jnp.concatenate([first_half, second_half])
    both_heads = jnp.stack(
        [
            jnp.where(is_target, own_heads, other_heads),
            jnp.where(is_target, other_heads, own_heads),
        ]
    )
    core_heads = from_other_core(both_heads)

    hidden_part = jnp.where(is_target, final_hidden[:part], final_hidden[part:]).astype(f32)

    block = captured.transpose(1, 0, 2).reshape(slab, layers * features)
    mine = copied(block, "y")
    other = from_other_core(mine)
    tokens = jnp.stack(
        [jnp.where(is_first, mine, other), jnp.where(is_first, other, mine)], axis=1
    ).reshape(-1, layers * features)
    partial = jnp.dot(
        tokens, unite_weight.reshape(layers * features, columns), preferred_element_type=f32
    )
    pieces = partial.astype(half).reshape(n_slabs, 2, part, columns).transpose(1, 0, 2, 3)
    received = exchanged(pieces.reshape(-1, part, columns), BLOCKS)
    united = jnp.sum(received.astype(f32), axis=0)

    squares = jnp.stack(
        [jnp.sum(hidden_part * hidden_part, axis=1), jnp.sum(united * united, axis=1)]
    )
    square_sums = jnp.sum(copied(squares, COLUMNS), axis=0)
    scales = lax.rsqrt(square_sums / model_width + EPSILON)
    target_part = (hidden_part * scales[0][:, None] * target_gain[None, :]).astype(bf16)
    draft_part = (united * scales[1][:, None] * draft_gain[None, :]).astype(bf16)
    both_rows = copied(jnp.stack([target_part, draft_part]), SLABS)
    draft_rows = both_rows[:, 1]
    other_rows = from_other_group(draft_rows)

    by_core = both_rows.reshape(n_y, 2, 2, part, columns)
    kept = jnp.where(is_first, by_core[:, 0], by_core[:, 1])
    given = jnp.where(is_first, by_core[:, 1], by_core[:, 0])
    taken = from_other_core(given)

    def share_of(rows, head):
        return jnp.einsum("ytd,vd->ytv", rows, head, preferred_element_type=f32)

    own_share = [share_of(kept[:, w], both_heads[w]) for w in range(2)]
    partials = jnp.stack(
        [
            (own_share[w] + share_of(taken[:, w], core_heads[w])).astype(half)
            for w in range(2)
        ],
        axis=1,
    )
    partials = exchanged(partials, "y")
    logits = jnp.sum(partials.astype(f32), axis=0)

    local_top = jnp.max(logits, axis=2)
    shifted = logits - local_top[:, :, None]
    raised = jnp.exp(shifted)
    local_total = jnp.sum(raised, axis=2)
    crossed = jnp.sum(raised[0] * shifted[1], axis=1)
    stats = copied(jnp.concatenate([local_top, local_total, crossed[None]]), SLABS)
    tops, totals, crosses = stats[:, 0:2], stats[:, 2:4], stats[:, 4]
    top = jnp.max(tops, axis=0)
    total = jnp.sum(totals * jnp.exp(tops - top[None]), axis=0)
    probs = jnp.exp(logits - top[:, :, None]) / total[:, :, None]
    block_factor = jnp.exp(tops[:, 0] - top[None, 0]) / total[None, 0]
    draft_shift = tops[:, 1] - top[None, 1] - jnp.log(total)[None, 1]
    cross_term = jnp.sum(block_factor * (crosses + totals[:, 0] * draft_shift), axis=0)
    other_term = from_other_group(cross_term)
    cross_term = jnp.concatenate(
        [
            jnp.where(is_target, cross_term, other_term),
            jnp.where(is_target, other_term, cross_term),
        ]
    )

    slab_index = lax.axis_index("y") * 2 + core
    valid_len = jnp.sum(
        jnp.where(lax.iota(jnp.int32, lengths.shape[0]) == slab_index, lengths, 0)
    )
    valid_mask = (lax.iota(jnp.int32, slab) < valid_len).astype(f32)
    valid_total = jnp.sum(lengths).astype(f32)
    token_loss = -valid_mask * cross_term

    weights = jnp.where(is_target, valid_mask[:part], valid_mask[part:]) / valid_total
    weighted = (probs[0] * weights[:, None]).astype(bf16)
    delta = ((probs[1] - probs[0]) * weights[:, None]).astype(bf16)
    outgoing = jnp.concatenate(
        [
            jnp.broadcast_to(weighted, (n_y, part, vocab)),
            jnp.broadcast_to(delta, (n_y, part, vocab)),
        ]
    )
    gathered = exchanged(outgoing, ("grp", "y"))
    core_gathered = from_other_core(gathered)

    all_rows = jnp.stack(
        [
            jnp.where(is_target, draft_rows, other_rows),
            jnp.where(is_target, other_rows, draft_rows),
        ]
    ).reshape(2, n_y, 2, part, columns)
    own_side = jnp.where(is_first, all_rows[:, :, 0], all_rows[:, :, 1])
    core_side = jnp.where(is_first, all_rows[:, :, 1], all_rows[:, :, 0])

    def gradient(weights_by_token, rows_by_token):
        return jnp.einsum(
            "tv,td->vd",
            weights_by_token.reshape(-1, vocab),
            rows_by_token.reshape(-1, columns),
            preferred_element_type=f32,
        )

    own_sums = gradient(gathered, own_side)
    summed = own_sums + gradient(core_gathered, core_side)
    sign_factor = jnp.where(is_target, -1.0, 1.0).astype(f32)
    grad_terms = (sign_factor * summed).astype(bf16)[None]
    return (grad_terms, token_loss)


def solution(mesh):
    sizes = mesh.shape
    grid = mesh.devices.reshape(sizes["grp"], 2, sizes["dp"] // 2, sizes["mp"] // 2, 2)
    fine = Mesh(grid, ("grp", "xl", "z", "y", "core"))
    in_specs = (
        P(None, COLUMNS, BLOCKS),
        P(None, BLOCKS, COLUMNS),
        P("grp", SLABS, COLUMNS),
        P(SLABS, COLUMNS),
        P(COLUMNS),
        P(COLUMNS),
        P(),
    )
    out_specs = (P("grp", SLABS, COLUMNS), P(COLUMNS))
    return jax.shard_map(
        per_device, mesh=fine, in_specs=in_specs, out_specs=out_specs, check_vma=False
    )
```

```python
import jax
import jax.numpy as jnp
from jax import lax
from jax.sharding import Mesh, PartitionSpec as P

EPSILON = 1e-05
SLABS = ("xl", "z")
BLOCKS = ("grp", "xl", "z")
COLUMNS = ("y", "core")


def exchanged(tiles, axes):
    return lax.all_to_all(tiles, axes, split_axis=0, concat_axis=0, tiled=True)


def copied(shard, axes):
    return exchanged(jnp.broadcast_to(shard, (lax.axis_size(axes), *shard.shape)), axes)


def from_other_core(shard):
    return lax.ppermute(shard, "core", [(0, 1), (1, 0)])


def from_other_group(shard):
    return lax.ppermute(shard, "grp", [(0, 1), (1, 0)])


def along_x(shard, step):
    n = lax.axis_size(("grp", "xl"))
    return lax.ppermute(shard, ("grp", "xl"), [(i, (i + step) % n) for i in range(n)])


def doubled(shard):
    pieces, stride = shard[None], lax.axis_size("z") // 2
    place = lax.axis_index("z")
    while stride:
        pairs = [(i, i ^ stride) for i in range(lax.axis_size("z"))]
        other = lax.ppermute(pieces, "z", pairs)
        low = (place & stride) == 0
        pieces = jnp.stack(
            [jnp.where(low, pieces, other), jnp.where(low, other, pieces)], axis=1
        ).reshape(-1, *shard.shape)
        stride //= 2
    other = lax.ppermute(pieces, "xl", [(0, 1), (1, 0)])
    low = lax.axis_index("xl") == 0
    return jnp.concatenate([jnp.where(low, pieces, other), jnp.where(low, other, pieces)])


def per_device(captured, unite_weight, heads, final_hidden, target_gain, draft_gain, lengths):
    f32, bf16, half = jnp.float32, jnp.bfloat16, jnp.float16
    columns = final_hidden.shape[1]
    model_width = columns * lax.axis_size(COLUMNS)
    layers, slab, features = captured.shape
    n_y = lax.axis_size("y")
    n_slabs = lax.axis_size(SLABS)
    part = slab // 2
    group = lax.axis_index("grp")
    core = lax.axis_index("core")
    is_target = group == 0
    is_first = core == 0
    vocab = heads.shape[1]

    own_heads = heads[0]
    first_half, second_half = own_heads[: vocab // 2], own_heads[vocab // 2 :]
    first_half = along_x(first_half, 1)
    second_half = along_x(second_half, -1)
    first_half = along_x(first_half, 1)
    second_half = along_x(second_half, -1)
    other_heads = jnp.concatenate([first_half, second_half])
    both_heads = jnp.stack(
        [
            jnp.where(is_target, own_heads, other_heads),
            jnp.where(is_target, other_heads, own_heads),
        ]
    )
    core_heads = from_other_core(both_heads)

    hidden_part = jnp.where(is_target, final_hidden[:part], final_hidden[part:])
    hidden_rows = doubled(hidden_part).astype(f32)

    block = captured.transpose(1, 0, 2).reshape(slab, layers * features)
    mine = copied(block, "y")
    other = from_other_core(mine)
    tokens = jnp.stack(
        [jnp.where(is_first, mine, other), jnp.where(is_first, other, mine)], axis=1
    ).reshape(-1, layers * features)
    partial = jnp.dot(
        tokens, unite_weight.reshape(layers * features, columns), preferred_element_type=f32
    )
    pieces = partial.astype(half).reshape(n_slabs, 2, part, columns).transpose(1, 0, 2, 3)
    received = exchanged(pieces.reshape(-1, part, columns), BLOCKS)
    united = jnp.sum(received.astype(f32), axis=0)

    squares = jnp.concatenate(
        [jnp.sum(hidden_rows * hidden_rows, axis=2), jnp.sum(united * united, axis=1)[None]]
    )
    squares = copied(squares, COLUMNS)
    scales = lax.rsqrt(jnp.sum(squares, axis=0) / model_width + EPSILON)
    draft_part = (united * scales[-1][:, None] * draft_gain[None, :]).astype(bf16)
    draft_rows = copied(draft_part, SLABS)
    other_rows = from_other_group(draft_rows)
    target_rows = (hidden_rows * scales[:-1][:, :, None] * target_gain).astype(bf16)

    def split_by_core(rows):
        by_core = rows.reshape(n_y, 2, part, columns)
        return (
            jnp.where(is_first, by_core[:, 0], by_core[:, 1]),
            jnp.where(is_first, by_core[:, 1], by_core[:, 0]),
        )

    def share_of(rows, head):
        return jnp.einsum("ytd,vd->ytv", rows, head, preferred_element_type=f32)

    kept, given = split_by_core(target_rows)
    taken = from_other_core(given)
    target_partial = (share_of(kept, both_heads[0]) + share_of(taken, core_heads[0])).astype(half)
    kept, given = split_by_core(draft_rows)
    taken = from_other_core(given)
    own_share = share_of(kept, both_heads[1])
    draft_partial = (own_share + share_of(taken, core_heads[1])).astype(half)
    partials = jnp.concatenate([target_partial, draft_partial], axis=1)
    partials = exchanged(partials, "y")
    logits = jnp.sum(partials.astype(f32), axis=0).reshape(2, part, vocab)

    local_top = jnp.max(logits, axis=2)
    shifted = logits - local_top[:, :, None]
    raised = jnp.exp(shifted)
    local_total = jnp.sum(raised, axis=2)
    crossed = jnp.sum(raised[0] * shifted[1], axis=1)
    stats = copied(jnp.concatenate([local_top, local_total, crossed[None]]), SLABS)
    tops, totals, crosses = stats[:, 0:2], stats[:, 2:4], stats[:, 4]
    top = jnp.max(tops, axis=0)
    total = jnp.sum(totals * jnp.exp(tops - top[None]), axis=0)
    probs = jnp.exp(logits - top[:, :, None]) / total[:, :, None]
    block_factor = jnp.exp(tops[:, 0] - top[None, 0]) / total[None, 0]
    draft_shift = tops[:, 1] - top[None, 1] - jnp.log(total)[None, 1]
    cross_term = jnp.sum(block_factor * (crosses + totals[:, 0] * draft_shift), axis=0)
    other_term = from_other_group(cross_term)
    cross_term = jnp.concatenate(
        [
            jnp.where(is_target, cross_term, other_term),
            jnp.where(is_target, other_term, cross_term),
        ]
    )

    slab_index = lax.axis_index("y") * 2 + core
    valid_len = jnp.sum(
        jnp.where(lax.iota(jnp.int32, lengths.shape[0]) == slab_index, lengths, 0)
    )
    valid_mask = (lax.iota(jnp.int32, slab) < valid_len).astype(f32)
    valid_total = jnp.sum(lengths).astype(f32)
    token_loss = -valid_mask * cross_term

    weights = jnp.where(is_target, valid_mask[:part], valid_mask[part:]) / valid_total
    weighted = (probs[0] * weights[:, None]).astype(bf16)
    delta = ((probs[1] - probs[0]) * weights[:, None]).astype(bf16)
    outgoing = jnp.concatenate(
        [
            jnp.broadcast_to(weighted, (n_y, part, vocab)),
            jnp.broadcast_to(delta, (n_y, part, vocab)),
        ]
    )
    gathered = exchanged(outgoing, ("grp", "y"))
    core_gathered = from_other_core(gathered)

    all_rows = jnp.stack(
        [jnp.where(is_target, draft_rows, other_rows), jnp.where(is_target, other_rows, draft_rows)]
    ).reshape(2, n_y, 2, part, columns)
    own_side = jnp.where(is_first, all_rows[:, :, 0], all_rows[:, :, 1])
    core_side = jnp.where(is_first, all_rows[:, :, 1], all_rows[:, :, 0])

    def gradient(weights_by_token, rows_by_token):
        return jnp.einsum(
            "tv,td->vd",
            weights_by_token.reshape(-1, vocab),
            rows_by_token.reshape(-1, columns),
            preferred_element_type=f32,
        )

    own_sums = gradient(gathered, own_side)
    summed = own_sums + gradient(core_gathered, core_side)
    sign_factor = jnp.where(is_target, -1.0, 1.0).astype(f32)
    grad_terms = (sign_factor * summed).astype(bf16)[None]
    return (grad_terms, token_loss)


def solution(mesh):
    sizes = mesh.shape
    grid = mesh.devices.reshape(sizes["grp"], 2, sizes["dp"] // 2, sizes["mp"] // 2, 2)
    fine = Mesh(grid, ("grp", "xl", "z", "y", "core"))
    in_specs = (
        P(None, COLUMNS, BLOCKS),
        P(None, BLOCKS, COLUMNS),
        P("grp", SLABS, COLUMNS),
        P(SLABS, COLUMNS),
        P(COLUMNS),
        P(COLUMNS),
        P(),
    )
    out_specs = (P("grp", SLABS, COLUMNS), P(COLUMNS))
    return jax.shard_map(
        per_device, mesh=fine, in_specs=in_specs, out_specs=out_specs, check_vma=False
    )
```

```python
import jax
import jax.numpy as jnp
from jax import lax
from jax.sharding import Mesh, PartitionSpec as P

EPSILON = 1e-05
SLABS = ("xl", "z")
BLOCKS = ("grp", "xl", "z")
COLUMNS = ("y", "core")


def exchanged(tiles, axes):
    return lax.all_to_all(tiles, axes, split_axis=0, concat_axis=0, tiled=True)


def copied(shard, axes):
    return exchanged(jnp.broadcast_to(shard, (lax.axis_size(axes), *shard.shape)), axes)


def from_other_core(shard):
    return lax.ppermute(shard, "core", [(0, 1), (1, 0)])


def from_other_group(shard):
    return lax.ppermute(shard, "grp", [(0, 1), (1, 0)])


def along_x(shard, step):
    n = lax.axis_size(("grp", "xl"))
    return lax.ppermute(shard, ("grp", "xl"), [(i, (i + step) % n) for i in range(n)])


def doubled(shard):
    pieces, stride = shard[None], lax.axis_size("z") // 2
    place = lax.axis_index("z")
    while stride:
        pairs = [(i, i ^ stride) for i in range(lax.axis_size("z"))]
        other = lax.ppermute(pieces, "z", pairs)
        low = (place & stride) == 0
        pieces = jnp.stack(
            [jnp.where(low, pieces, other), jnp.where(low, other, pieces)], axis=1
        ).reshape(-1, *shard.shape)
        stride //= 2
    other = lax.ppermute(pieces, "xl", [(0, 1), (1, 0)])
    low = lax.axis_index("xl") == 0
    return jnp.concatenate([jnp.where(low, pieces, other), jnp.where(low, other, pieces)])


def per_device(captured, unite_weight, heads, final_hidden, target_gain, draft_gain, lengths):
    f32, bf16, half = jnp.float32, jnp.bfloat16, jnp.float16
    columns = final_hidden.shape[1]
    model_width = columns * lax.axis_size(COLUMNS)
    layers, slab, features = captured.shape
    n_y = lax.axis_size("y")
    part = slab // 2
    group = lax.axis_index("grp")
    core = lax.axis_index("core")
    is_target = group == 0
    is_first = core == 0
    vocab = heads.shape[1]

    own_heads = heads[0]
    first_half, second_half = own_heads[: vocab // 2], own_heads[vocab // 2 :]
    first_half = along_x(first_half, 1)
    second_half = along_x(second_half, -1)
    first_half = along_x(first_half, 1)
    second_half = along_x(second_half, -1)
    other_heads = jnp.concatenate([first_half, second_half])
    both_heads = jnp.stack(
        [
            jnp.where(is_target, own_heads, other_heads),
            jnp.where(is_target, other_heads, own_heads),
        ]
    )
    core_heads = from_other_core(both_heads)

    hidden_part = jnp.where(is_target, final_hidden[:part], final_hidden[part:])
    hidden_rows = doubled(hidden_part).astype(f32)

    block = captured.transpose(1, 0, 2).reshape(slab, layers * features)
    mine = copied(block, "y")
    other = from_other_core(mine)
    tokens = jnp.stack(
        [jnp.where(is_first, mine, other), jnp.where(is_first, other, mine)], axis=1
    ).reshape(-1, layers * features)
    partial = jnp.dot(
        tokens, unite_weight.reshape(layers * features, columns), preferred_element_type=f32
    )
    pieces = partial.astype(half).reshape(-1, part, columns)
    received = exchanged(pieces, (*SLABS, "grp"))
    united = jnp.sum(received.astype(f32), axis=0)

    squares = jnp.concatenate(
        [jnp.sum(hidden_rows * hidden_rows, axis=2), jnp.sum(united * united, axis=1)[None]]
    )
    squares = copied(squares, COLUMNS)
    scales = lax.rsqrt(jnp.sum(squares, axis=0) / model_width + EPSILON)
    draft_part = (united * scales[-1][:, None] * draft_gain[None, :]).astype(bf16)
    draft_rows = copied(draft_part, SLABS)
    other_rows = from_other_group(draft_rows)
    target_rows = (hidden_rows * scales[:-1][:, :, None] * target_gain).astype(bf16)

    def split_by_core(rows):
        by_core = rows.reshape(n_y, 2, part, columns)
        return (
            jnp.where(is_first, by_core[:, 0], by_core[:, 1]),
            jnp.where(is_first, by_core[:, 1], by_core[:, 0]),
        )

    def share_of(rows, head):
        return jnp.einsum("ytd,vd->ytv", rows, head, preferred_element_type=f32)

    kept, given = split_by_core(target_rows)
    taken = from_other_core(given)
    target_partial = (
        share_of(kept, both_heads[0]) + share_of(taken, core_heads[0])
    ).astype(half)
    kept, given = split_by_core(draft_rows)
    taken = from_other_core(given)
    own_share = share_of(kept, both_heads[1])
    draft_partial = (own_share + share_of(taken, core_heads[1])).astype(half)
    partials = jnp.concatenate([target_partial, draft_partial], axis=1)
    partials = exchanged(partials, "y")
    logits = jnp.sum(partials.astype(f32), axis=0).reshape(2, part, vocab)

    local_top = jnp.max(logits, axis=2)
    shifted = logits - local_top[:, :, None]
    raised = jnp.exp(shifted)
    local_total = jnp.sum(raised, axis=2)
    crossed = jnp.sum(raised[0] * shifted[1], axis=1)
    stats = copied(jnp.concatenate([local_top, local_total, crossed[None]]), SLABS)
    tops, totals, crosses = stats[:, 0:2], stats[:, 2:4], stats[:, 4]
    top = jnp.max(tops, axis=0)
    total = jnp.sum(totals * jnp.exp(tops - top[None]), axis=0)
    probs = jnp.exp(logits - top[:, :, None]) / total[:, :, None]
    block_factor = jnp.exp(tops[:, 0] - top[None, 0]) / total[None, 0]
    draft_shift = tops[:, 1] - top[None, 1] - jnp.log(total)[None, 1]
    cross_term = jnp.sum(block_factor * (crosses + totals[:, 0] * draft_shift), axis=0)
    other_term = from_other_group(cross_term)
    cross_term = jnp.concatenate(
        [
            jnp.where(is_target, cross_term, other_term),
            jnp.where(is_target, other_term, cross_term),
        ]
    )

    slab_index = lax.axis_index("y") * 2 + core
    valid_len = jnp.sum(
        jnp.where(lax.iota(jnp.int32, lengths.shape[0]) == slab_index, lengths, 0)
    )
    valid_mask = (lax.iota(jnp.int32, slab) < valid_len).astype(f32)
    valid_total = jnp.sum(lengths).astype(f32)
    token_loss = -valid_mask * cross_term

    weights = jnp.where(is_target, valid_mask[:part], valid_mask[part:]) / valid_total
    weighted = (probs[0] * weights[:, None]).astype(bf16)
    delta = ((probs[1] - probs[0]) * weights[:, None]).astype(bf16)
    outgoing = jnp.broadcast_to(
        jnp.stack([weighted, delta])[:, None], (2, n_y, part, vocab)
    ).reshape(-1, part, vocab)
    gathered = exchanged(outgoing, ("grp", "y"))
    core_gathered = from_other_core(gathered)

    all_rows = jnp.stack(
        [
            jnp.where(is_target, draft_rows, other_rows),
            jnp.where(is_target, other_rows, draft_rows),
        ]
    ).reshape(2, n_y, 2, part, columns)
    own_side = jnp.where(is_first, all_rows[:, :, 0], all_rows[:, :, 1])
    core_side = jnp.where(is_first, all_rows[:, :, 1], all_rows[:, :, 0])

    def gradient(weights_by_token, rows_by_token):
        return jnp.einsum(
            "tv,td->vd",
            weights_by_token.reshape(-1, vocab),
            rows_by_token.reshape(-1, columns),
            preferred_element_type=f32,
        )

    own_sums = gradient(gathered, own_side)
    summed = own_sums + gradient(core_gathered, core_side)
    sign_factor = jnp.where(is_target, -1.0, 1.0).astype(f32)
    grad_terms = (sign_factor * summed).astype(bf16)[None]
    return (grad_terms, token_loss)


def solution(mesh):
    sizes = mesh.shape
    grid = mesh.devices.reshape(sizes["grp"], 2, sizes["dp"] // 2, sizes["mp"] // 2, 2)
    fine = Mesh(grid, ("grp", "xl", "z", "y", "core"))
    in_specs = (
        P(None, COLUMNS, BLOCKS),
        P(None, BLOCKS, COLUMNS),
        P("grp", SLABS, COLUMNS),
        P(SLABS, COLUMNS),
        P(COLUMNS),
        P(COLUMNS),
        P(),
    )
    out_specs = (P("grp", SLABS, COLUMNS), P(COLUMNS))
    return jax.shard_map(
        per_device, mesh=fine, in_specs=in_specs, out_specs=out_specs, check_vma=False
    )
```

```python
import jax
import jax.numpy as jnp
from jax import lax
from jax.sharding import Mesh, PartitionSpec as P

EPSILON = 1e-05
SLABS = ("xl", "z")
BLOCKS = ("grp", "xl", "z")
COLUMNS = ("y", "core")


def exchanged(tiles, axes):
    return lax.all_to_all(tiles, axes, split_axis=0, concat_axis=0, tiled=True)


def copied(shard, axes):
    return exchanged(jnp.broadcast_to(shard, (lax.axis_size(axes), *shard.shape)), axes)


def from_other_core(shard):
    return lax.ppermute(shard, "core", [(0, 1), (1, 0)])


def from_other_group(shard):
    return lax.ppermute(shard, "grp", [(0, 1), (1, 0)])


def along_x(shard, step):
    n = lax.axis_size(("grp", "xl"))
    return lax.ppermute(shard, ("grp", "xl"), [(i, (i + step) % n) for i in range(n)])


def doubled(shard):
    pieces, stride = shard[None], lax.axis_size("z") // 2
    place = lax.axis_index("z")
    while stride:
        pairs = [(i, i ^ stride) for i in range(lax.axis_size("z"))]
        other = lax.ppermute(pieces, "z", pairs)
        low = (place & stride) == 0
        pieces = jnp.stack(
            [jnp.where(low, pieces, other), jnp.where(low, other, pieces)], axis=1
        ).reshape(-1, *shard.shape)
        stride //= 2
    return pieces


def copied_small(table, axes):
    rows, lanes = table.shape
    tile = jnp.pad(table, ((0, -rows % 8), (0, -lanes % 128)))
    return copied(tile, axes)[:, :rows, :lanes]


def per_device(captured, unite_weight, heads, final_hidden, target_gain, draft_gain, lengths):
    f32, bf16, half = jnp.float32, jnp.bfloat16, jnp.float16
    columns = final_hidden.shape[1]
    model_width = columns * lax.axis_size(COLUMNS)
    layers, slab, features = captured.shape
    n_y = lax.axis_size("y")
    part = slab // 2
    group = lax.axis_index("grp")
    core = lax.axis_index("core")
    is_target = group == 0
    is_first = core == 0
    vocab = heads.shape[1]

    own_heads = heads[0]
    first_half, second_half = own_heads[: vocab // 2], own_heads[vocab // 2 :]
    first_half = along_x(first_half, 1)
    second_half = along_x(second_half, -1)
    first_half = along_x(first_half, 1)
    second_half = along_x(second_half, -1)
    other_heads = jnp.concatenate([first_half, second_half])
    both_heads = jnp.stack(
        [
            jnp.where(is_target, own_heads, other_heads),
            jnp.where(is_target, other_heads, own_heads),
        ]
    )
    core_heads = from_other_core(both_heads)

    hidden_part = jnp.where(is_target, final_hidden[:part], final_hidden[part:])
    hidden_rows = doubled(hidden_part).astype(f32)

    block = captured.transpose(1, 0, 2).reshape(slab, layers * features)
    mine = copied(block, "y")
    other = from_other_core(mine)
    tokens = jnp.stack(
        [jnp.where(is_first, mine, other), jnp.where(is_first, other, mine)], axis=1
    ).reshape(-1, layers * features)
    partial = jnp.dot(
        tokens, unite_weight.reshape(layers * features, columns), preferred_element_type=f32
    )
    pieces = partial.astype(half).reshape(-1, part, columns)
    received = exchanged(pieces, (*SLABS, "grp"))
    united = jnp.sum(received.astype(f32), axis=0)

    squares = jnp.concatenate(
        [jnp.sum(hidden_rows * hidden_rows, axis=2), jnp.sum(united * united, axis=1)[None]]
    )
    squares = copied_small(squares, COLUMNS)
    scales = lax.rsqrt(jnp.sum(squares, axis=0) / model_width + EPSILON)
    draft_part = (united * scales[-1][:, None] * draft_gain[None, :]).astype(bf16)
    draft_rows = copied(draft_part, SLABS)
    other_rows = from_other_group(draft_rows)
    target_rows = (hidden_rows * scales[:-1][:, :, None] * target_gain).astype(bf16)
    other_target = lax.ppermute(target_rows, "xl", [(0, 1), (1, 0)])
    is_low = lax.axis_index("xl") == 0
    target_rows = jnp.concatenate(
        [
            jnp.where(is_low, target_rows, other_target),
            jnp.where(is_low, other_target, target_rows),
        ]
    )

    def split_by_core(rows):
        by_core = rows.reshape(n_y, 2, part, columns)
        return (
            jnp.where(is_first, by_core[:, 0], by_core[:, 1]),
            jnp.where(is_first, by_core[:, 1], by_core[:, 0]),
        )

    def share_of(rows, head):
        return jnp.einsum("ytd,vd->ytv", rows, head, preferred_element_type=f32)

    kept, given = split_by_core(target_rows)
    taken = from_other_core(given)
    target_partial = (
        share_of(kept, both_heads[0]) + share_of(taken, core_heads[0])
    ).astype(half)
    kept, given = split_by_core(draft_rows)
    taken = from_other_core(given)
    own_share = share_of(kept, both_heads[1])
    draft_partial = (own_share + share_of(taken, core_heads[1])).astype(half)
    partials = jnp.concatenate([target_partial, draft_partial], axis=1)
    partials = exchanged(partials, "y")
    logits = jnp.sum(partials.astype(f32), axis=0).reshape(2, part, vocab)

    local_top = jnp.max(logits, axis=2)
    shifted = logits - local_top[:, :, None]
    raised = jnp.exp(shifted)
    local_total = jnp.sum(raised, axis=2)
    crossed = jnp.sum(raised[0] * shifted[1], axis=1)
    stats = copied_small(jnp.concatenate([local_top, local_total, crossed[None]]), SLABS)
    tops, totals, crosses = stats[:, 0:2], stats[:, 2:4], stats[:, 4]
    top = jnp.max(tops, axis=0)
    total = jnp.sum(totals * jnp.exp(tops - top[None]), axis=0)
    probs = jnp.exp(logits - top[:, :, None]) / total[:, :, None]
    block_factor = jnp.exp(tops[:, 0] - top[None, 0]) / total[None, 0]
    draft_shift = tops[:, 1] - top[None, 1] - jnp.log(total)[None, 1]
    cross_term = jnp.sum(block_factor * (crosses + totals[:, 0] * draft_shift), axis=0)
    other_term = from_other_group(cross_term)
    cross_term = jnp.concatenate(
        [
            jnp.where(is_target, cross_term, other_term),
            jnp.where(is_target, other_term, cross_term),
        ]
    )

    slab_index = lax.axis_index("y") * 2 + core
    valid_len = jnp.sum(
        jnp.where(lax.iota(jnp.int32, lengths.shape[0]) == slab_index, lengths, 0)
    )
    valid_mask = (lax.iota(jnp.int32, slab) < valid_len).astype(f32)
    valid_total = jnp.sum(lengths).astype(f32)
    token_loss = -valid_mask * cross_term

    weights = jnp.where(is_target, valid_mask[:part], valid_mask[part:]) / valid_total
    weighted = (probs[0] * weights[:, None]).astype(bf16)
    delta = ((probs[1] - probs[0]) * weights[:, None]).astype(bf16)
    outgoing = jnp.broadcast_to(
        jnp.stack([weighted, delta])[:, None], (2, n_y, part, vocab)
    ).reshape(-1, part, vocab)
    gathered = exchanged(outgoing, ("grp", "y"))
    core_gathered = from_other_core(gathered)

    all_rows = jnp.stack(
        [
            jnp.where(is_target, draft_rows, other_rows),
            jnp.where(is_target, other_rows, draft_rows),
        ]
    ).reshape(2, n_y, 2, part, columns)
    own_side = jnp.where(is_first, all_rows[:, :, 0], all_rows[:, :, 1])
    core_side = jnp.where(is_first, all_rows[:, :, 1], all_rows[:, :, 0])

    def gradient(weights_by_token, rows_by_token):
        return jnp.einsum(
            "tv,td->vd",
            weights_by_token.reshape(-1, vocab),
            rows_by_token.reshape(-1, columns),
            preferred_element_type=f32,
        )

    own_sums = gradient(gathered, own_side)
    summed = own_sums + gradient(core_gathered, core_side)
    sign_factor = jnp.where(is_target, -1.0, 1.0).astype(f32)
    grad_terms = (sign_factor * summed).astype(bf16)[None]
    return (grad_terms, token_loss)


def solution(mesh):
    sizes = mesh.shape
    grid = mesh.devices.reshape(sizes["grp"], 2, sizes["dp"] // 2, sizes["mp"] // 2, 2)
    fine = Mesh(grid, ("grp", "xl", "z", "y", "core"))
    in_specs = (
        P(None, COLUMNS, BLOCKS),
        P(None, BLOCKS, COLUMNS),
        P("grp", SLABS, COLUMNS),
        P(SLABS, COLUMNS),
        P(COLUMNS),
        P(COLUMNS),
        P(),
    )
    out_specs = (P("grp", SLABS, COLUMNS), P(COLUMNS))
    return jax.shard_map(
        per_device, mesh=fine, in_specs=in_specs, out_specs=out_specs, check_vma=False
    )
```

```python
import jax
import jax.numpy as jnp
from jax import lax
from jax.sharding import Mesh, PartitionSpec as P

EPSILON = 1e-05
SLABS = ("xl", "z")
BLOCKS = ("grp", "xl", "z")
COLUMNS = ("y", "core")


def exchanged(tiles, axes):
    return lax.all_to_all(tiles, axes, split_axis=0, concat_axis=0, tiled=True)


def copied(shard, axes):
    return exchanged(jnp.broadcast_to(shard, (lax.axis_size(axes), *shard.shape)), axes)


def from_other_core(shard):
    return lax.ppermute(shard, "core", [(0, 1), (1, 0)])


def from_other_group(shard):
    return lax.ppermute(shard, "grp", [(0, 1), (1, 0)])


def along_x(shard, step):
    n = lax.axis_size(("grp", "xl"))
    return lax.ppermute(shard, ("grp", "xl"), [(i, (i + step) % n) for i in range(n)])


def doubled(shard):
    pieces, stride = shard[None], lax.axis_size("z") // 2
    place = lax.axis_index("z")
    while stride:
        pairs = [(i, i ^ stride) for i in range(lax.axis_size("z"))]
        other = lax.ppermute(pieces, "z", pairs)
        low = (place & stride) == 0
        pieces = jnp.stack(
            [jnp.where(low, pieces, other), jnp.where(low, other, pieces)], axis=1
        ).reshape(-1, *shard.shape)
        stride //= 2
    other = lax.ppermute(pieces, "xl", [(0, 1), (1, 0)])
    low = lax.axis_index("xl") == 0
    return jnp.concatenate([jnp.where(low, pieces, other), jnp.where(low, other, pieces)])


def copied_small(table, axes):
    rows, lanes = table.shape
    tile = jnp.pad(table, ((0, -rows % 8), (0, -lanes % 128)))
    return copied(tile, axes)[:, :rows, :lanes]


def per_device(captured, unite_weight, heads, final_hidden, target_gain, draft_gain, lengths):
    f32, bf16, half = jnp.float32, jnp.bfloat16, jnp.float16
    columns = final_hidden.shape[1]
    model_width = columns * lax.axis_size(COLUMNS)
    layers, slab, features = captured.shape
    n_y = lax.axis_size("y")
    part = slab // 2
    group = lax.axis_index("grp")
    core = lax.axis_index("core")
    is_target = group == 0
    is_first = core == 0
    vocab = heads.shape[1]

    own_heads = heads[0]
    first_half, second_half = own_heads[: vocab // 2], own_heads[vocab // 2 :]
    first_half = along_x(first_half, 1)
    second_half = along_x(second_half, -1)
    first_half = along_x(first_half, 1)
    second_half = along_x(second_half, -1)
    other_heads = jnp.concatenate([first_half, second_half])
    both_heads = jnp.stack(
        [
            jnp.where(is_target, own_heads, other_heads),
            jnp.where(is_target, other_heads, own_heads),
        ]
    )
    core_heads = from_other_core(both_heads)

    hidden_part = jnp.where(is_target, final_hidden[:part], final_hidden[part:])
    hidden_rows = doubled(hidden_part).astype(f32)

    block = captured.transpose(1, 0, 2).reshape(slab, layers * features)
    mine = copied(block, "y")
    other = from_other_core(mine)
    tokens = jnp.stack(
        [jnp.where(is_first, mine, other), jnp.where(is_first, other, mine)], axis=1
    ).reshape(-1, layers * features)
    partial = jnp.dot(
        tokens, unite_weight.reshape(layers * features, columns), preferred_element_type=f32
    )
    pieces = partial.astype(half).reshape(-1, part, columns)
    received = exchanged(pieces, (*SLABS, "grp"))
    united = jnp.sum(received.astype(f32), axis=0)

    united_squares = jnp.pad(jnp.sum(united * united, axis=1), (0, 128 - part))
    squares = jnp.concatenate(
        [jnp.sum(hidden_rows * hidden_rows, axis=2).reshape(-1, 128), united_squares[None]]
    )
    squares = copied_small(squares, COLUMNS)
    scales = lax.rsqrt(jnp.sum(squares, axis=0) / model_width + EPSILON)
    draft_part = (united * scales[-1, :part, None] * draft_gain[None, :]).astype(bf16)
    hidden_scale = scales[:-1].reshape(-1, part, 1)
    draft_rows = copied(draft_part, SLABS)
    other_rows = from_other_group(draft_rows)
    target_rows = (hidden_rows * hidden_scale * target_gain).astype(bf16)

    def split_by_core(rows):
        by_core = rows.reshape(n_y, 2, part, columns)
        return (
            jnp.where(is_first, by_core[:, 0], by_core[:, 1]),
            jnp.where(is_first, by_core[:, 1], by_core[:, 0]),
        )

    def share_of(rows, head):
        return jnp.einsum("ytd,vd->ytv", rows, head, preferred_element_type=f32)

    kept, given = split_by_core(target_rows)
    taken = from_other_core(given)
    target_partial = (share_of(kept, both_heads[0]) + share_of(taken, core_heads[0])).astype(half)
    kept, given = split_by_core(draft_rows)
    taken = from_other_core(given)
    own_share = share_of(kept, both_heads[1])
    draft_partial = (own_share + share_of(taken, core_heads[1])).astype(half)
    partials = jnp.concatenate([target_partial, draft_partial], axis=1)
    partials = exchanged(partials, "y")
    logits = jnp.sum(partials.astype(f32), axis=0).reshape(2, part, vocab)

    local_top = jnp.max(logits, axis=2)
    shifted = logits - local_top[:, :, None]
    raised = jnp.exp(shifted)
    local_total = jnp.sum(raised, axis=2)
    crossed = jnp.sum(raised[0] * shifted[1], axis=1)
    stats = copied_small(jnp.concatenate([local_top, local_total, crossed[None]]), SLABS)
    tops, totals, crosses = stats[:, 0:2], stats[:, 2:4], stats[:, 4]
    top = jnp.max(tops, axis=0)
    total = jnp.sum(totals * jnp.exp(tops - top[None]), axis=0)
    probs = jnp.exp(logits - top[:, :, None]) / total[:, :, None]
    block_factor = jnp.exp(tops[:, 0] - top[None, 0]) / total[None, 0]
    draft_shift = tops[:, 1] - top[None, 1] - jnp.log(total)[None, 1]
    cross_term = jnp.sum(block_factor * (crosses + totals[:, 0] * draft_shift), axis=0)
    other_term = from_other_group(cross_term)
    cross_term = jnp.concatenate(
        [
            jnp.where(is_target, cross_term, other_term),
            jnp.where(is_target, other_term, cross_term),
        ]
    )

    slab_index = lax.axis_index("y") * 2 + core
    valid_len = jnp.sum(
        jnp.where(lax.iota(jnp.int32, lengths.shape[0]) == slab_index, lengths, 0)
    )
    valid_mask = (lax.iota(jnp.int32, slab) < valid_len).astype(f32)
    valid_total = jnp.sum(lengths).astype(f32)
    token_loss = -valid_mask * cross_term

    weights = jnp.where(is_target, valid_mask[:part], valid_mask[part:]) / valid_total
    weighted = (probs[0] * weights[:, None]).astype(bf16)
    delta = ((probs[1] - probs[0]) * weights[:, None]).astype(bf16)
    outgoing = jnp.broadcast_to(
        jnp.stack([weighted, delta])[:, None], (2, n_y, part, vocab)
    ).reshape(-1, part, vocab)
    gathered = exchanged(outgoing, ("grp", "y"))
    core_gathered = from_other_core(gathered)

    all_rows = jnp.stack(
        [jnp.where(is_target, draft_rows, other_rows), jnp.where(is_target, other_rows, draft_rows)]
    ).reshape(2, n_y, 2, part, columns)
    own_side = jnp.where(is_first, all_rows[:, :, 0], all_rows[:, :, 1])
    core_side = jnp.where(is_first, all_rows[:, :, 1], all_rows[:, :, 0])

    def gradient(weights_by_token, rows_by_token):
        return jnp.einsum(
            "tv,td->vd",
            weights_by_token.reshape(-1, vocab),
            rows_by_token.reshape(-1, columns),
            preferred_element_type=f32,
        )

    own_sums = gradient(gathered, own_side)
    summed = own_sums + gradient(core_gathered, core_side)
    sign_factor = jnp.where(is_target, -1.0, 1.0).astype(f32)
    grad_terms = (sign_factor * summed).astype(bf16)[None]
    return (grad_terms, token_loss)


def solution(mesh):
    sizes = mesh.shape
    grid = mesh.devices.reshape(sizes["grp"], 2, sizes["dp"] // 2, sizes["mp"] // 2, 2)
    fine = Mesh(grid, ("grp", "xl", "z", "y", "core"))
    in_specs = (
        P(None, COLUMNS, BLOCKS),
        P(None, BLOCKS, COLUMNS),
        P("grp", SLABS, COLUMNS),
        P(SLABS, COLUMNS),
        P(COLUMNS),
        P(COLUMNS),
        P(),
    )
    out_specs = (P("grp", SLABS, COLUMNS), P(COLUMNS))
    return jax.shard_map(
        per_device, mesh=fine, in_specs=in_specs, out_specs=out_specs, check_vma=False
    )
```

```python
import jax
import jax.numpy as jnp
from jax import lax
from jax.sharding import Mesh, PartitionSpec as P

EPSILON = 1e-05
SLABS = ("xl", "z")
BLOCKS = ("grp", "xl", "z")
COLUMNS = ("y", "core")


def exchanged(tiles, axes):
    return lax.all_to_all(tiles, axes, split_axis=0, concat_axis=0, tiled=True)


def copied(shard, axes):
    return exchanged(jnp.broadcast_to(shard, (lax.axis_size(axes), *shard.shape)), axes)


def from_other_core(shard):
    return lax.ppermute(shard, "core", [(0, 1), (1, 0)])


def from_other_group(shard):
    return lax.ppermute(shard, "grp", [(0, 1), (1, 0)])


def along_x(shard, step):
    n = lax.axis_size(("grp", "xl"))
    return lax.ppermute(shard, ("grp", "xl"), [(i, (i + step) % n) for i in range(n)])


def doubled(shard):
    pieces, stride = shard[None], lax.axis_size("z") // 2
    place = lax.axis_index("z")
    while stride:
        pairs = [(i, i ^ stride) for i in range(lax.axis_size("z"))]
        other = lax.ppermute(pieces, "z", pairs)
        low = (place & stride) == 0
        pieces = jnp.stack(
            [jnp.where(low, pieces, other), jnp.where(low, other, pieces)], axis=1
        ).reshape(-1, *shard.shape)
        stride //= 2
    other = lax.ppermute(pieces, "xl", [(0, 1), (1, 0)])
    low = lax.axis_index("xl") == 0
    return jnp.concatenate([jnp.where(low, pieces, other), jnp.where(low, other, pieces)])


def copied_small(table, axes):
    rows, lanes = table.shape
    tile = jnp.pad(table, ((0, -rows % 8), (0, -lanes % 128)))
    return copied(tile, axes)[:, :rows, :lanes]


def per_device(captured, unite_weight, heads, final_hidden, target_gain, draft_gain, lengths):
    f32, bf16, half = jnp.float32, jnp.bfloat16, jnp.float16
    columns = final_hidden.shape[1]
    model_width = columns * lax.axis_size(COLUMNS)
    layers, slab, features = captured.shape
    n_y = lax.axis_size("y")
    part = slab // 2
    group = lax.axis_index("grp")
    core = lax.axis_index("core")
    is_target = group == 0
    is_first = core == 0
    vocab = heads.shape[1]

    own_heads = heads[0]
    first_half, second_half = own_heads[: vocab // 2], own_heads[vocab // 2 :]
    first_half = along_x(first_half, 1)
    second_half = along_x(second_half, -1)
    first_half = along_x(first_half, 1)
    second_half = along_x(second_half, -1)
    other_heads = jnp.concatenate([first_half, second_half])
    target_head = jnp.where(is_target, own_heads, other_heads)
    draft_head = jnp.where(is_target, other_heads, own_heads)
    core_target_head = from_other_core(target_head)
    core_draft_head = from_other_core(draft_head)

    hidden_part = jnp.where(is_target, final_hidden[:part], final_hidden[part:])
    hidden_rows = doubled(hidden_part).astype(f32)

    block = captured.transpose(1, 0, 2).reshape(slab, layers * features)
    mine = copied(block, "y")
    other = from_other_core(mine)
    tokens = jnp.stack(
        [jnp.where(is_first, mine, other), jnp.where(is_first, other, mine)], axis=1
    ).reshape(-1, layers * features)
    partial = jnp.dot(
        tokens, unite_weight.reshape(layers * features, columns), preferred_element_type=f32
    )
    pieces = partial.astype(half).reshape(-1, part, columns)
    received = exchanged(pieces, (*SLABS, "grp"))
    united = jnp.sum(received.astype(f32), axis=0)

    united_squares = jnp.pad(jnp.sum(united * united, axis=1), (0, 128 - part))
    squares = jnp.concatenate(
        [jnp.sum(hidden_rows * hidden_rows, axis=2).reshape(-1, 128), united_squares[None]]
    )
    squares = copied_small(squares, COLUMNS)
    scales = lax.rsqrt(jnp.sum(squares, axis=0) / model_width + EPSILON)
    draft_part = (united * scales[-1, :part, None] * draft_gain[None, :]).astype(bf16)
    hidden_scale = scales[:-1].reshape(-1, part, 1)
    draft_rows = copied(draft_part, SLABS)
    other_rows = from_other_group(draft_rows)
    target_rows = (hidden_rows * hidden_scale * target_gain).astype(bf16)

    def split_by_core(rows):
        by_core = rows.reshape(n_y, 2, part, columns)
        return (
            jnp.where(is_first, by_core[:, 0], by_core[:, 1]),
            jnp.where(is_first, by_core[:, 1], by_core[:, 0]),
        )

    def share_of(rows, head):
        return jnp.einsum("ytd,vd->ytv", rows, head, preferred_element_type=f32)

    kept, given = split_by_core(target_rows)
    taken = from_other_core(given)
    target_partial = (share_of(kept, target_head) + share_of(taken, core_target_head)).astype(half)
    core_rows = from_other_core(draft_rows)
    kept, taken = split_by_core(draft_rows)[0], split_by_core(core_rows)[0]
    own_share = share_of(kept, draft_head)
    draft_partial = (own_share + share_of(taken, core_draft_head)).astype(half)
    partials = jnp.concatenate([target_partial, draft_partial], axis=1)
    partials = exchanged(partials, "y")
    logits = jnp.sum(partials.astype(f32), axis=0).reshape(2, part, vocab)

    local_top = jnp.max(logits, axis=2)
    shifted = logits - local_top[:, :, None]
    raised = jnp.exp(shifted)
    local_total = jnp.sum(raised, axis=2)
    crossed = jnp.sum(raised[0] * shifted[1], axis=1)
    stats = copied_small(jnp.concatenate([local_top, local_total, crossed[None]]), SLABS)
    tops, totals, crosses = stats[:, 0:2], stats[:, 2:4], stats[:, 4]
    top = jnp.max(tops, axis=0)
    total = jnp.sum(totals * jnp.exp(tops - top[None]), axis=0)
    probs = jnp.exp(logits - top[:, :, None]) / total[:, :, None]
    block_factor = jnp.exp(tops[:, 0] - top[None, 0]) / total[None, 0]
    draft_shift = tops[:, 1] - top[None, 1] - jnp.log(total)[None, 1]
    cross_term = jnp.sum(block_factor * (crosses + totals[:, 0] * draft_shift), axis=0)
    other_term = from_other_group(cross_term)
    cross_term = jnp.concatenate(
        [
            jnp.where(is_target, cross_term, other_term),
            jnp.where(is_target, other_term, cross_term),
        ]
    )

    slab_index = lax.axis_index("y") * 2 + core
    valid_len = jnp.sum(
        jnp.where(lax.iota(jnp.int32, lengths.shape[0]) == slab_index, lengths, 0)
    )
    valid_mask = (lax.iota(jnp.int32, slab) < valid_len).astype(f32)
    valid_total = jnp.sum(lengths).astype(f32)
    token_loss = -valid_mask * cross_term

    weights = jnp.where(is_target, valid_mask[:part], valid_mask[part:]) / valid_total
    weighted = (probs[0] * weights[:, None]).astype(bf16)
    delta = ((probs[1] - probs[0]) * weights[:, None]).astype(bf16)
    outgoing = jnp.broadcast_to(
        jnp.stack([weighted, delta])[:, None], (2, n_y, part, vocab)
    ).reshape(-1, part, vocab)
    gathered = exchanged(outgoing, ("grp", "y"))
    core_gathered = from_other_core(gathered)

    all_rows = jnp.stack(
        [jnp.where(is_target, draft_rows, other_rows), jnp.where(is_target, other_rows, draft_rows)]
    ).reshape(2, n_y, 2, part, columns)
    own_side = jnp.where(is_first, all_rows[:, :, 0], all_rows[:, :, 1])
    core_side = jnp.where(is_first, all_rows[:, :, 1], all_rows[:, :, 0])

    def gradient(weights_by_token, rows_by_token):
        return jnp.einsum(
            "tv,td->vd",
            weights_by_token.reshape(-1, vocab),
            rows_by_token.reshape(-1, columns),
            preferred_element_type=f32,
        )

    own_sums = gradient(gathered, own_side)
    summed = own_sums + gradient(core_gathered, core_side)
    sign_factor = jnp.where(is_target, -1.0, 1.0).astype(f32)
    grad_terms = (sign_factor * summed).astype(bf16)[None]
    return (grad_terms, token_loss)


def solution(mesh):
    sizes = mesh.shape
    grid = mesh.devices.reshape(sizes["grp"], 2, sizes["dp"] // 2, sizes["mp"] // 2, 2)
    fine = Mesh(grid, ("grp", "xl", "z", "y", "core"))
    in_specs = (
        P(None, COLUMNS, BLOCKS),
        P(None, BLOCKS, COLUMNS),
        P("grp", SLABS, COLUMNS),
        P(SLABS, COLUMNS),
        P(COLUMNS),
        P(COLUMNS),
        P(),
    )
    out_specs = (P("grp", SLABS, COLUMNS), P(COLUMNS))
    return jax.shard_map(
        per_device, mesh=fine, in_specs=in_specs, out_specs=out_specs, check_vma=False
    )
```
